32 devices in a mesh: gx: 4 (over y, x), gy: 8 (over z, core).
Axes of the slice: x: 2, y: 2, z: 4, core: 2. Of those that a mesh axis runs over, the one named last changes fastest.
Arguments:
- state: float32 [5, 64, 128, 1024], P(None, None, 'gx', 'gy'), may hold values from -4 to 4
- parent_slots: float32 [16, 5, 64, 16, 128], P('gy'), may hold values from -6 to 6
- block_rows: int32 [16], replicated, may hold values from 1 to 128, 1024 in all
- block_slot: int32 [16], replicated, may hold values from 0 to 15, each once
- nest_shift: int32 [1], replicated, may hold values from 1 to 16
- sound_speed2: float32 [64], replicated, may hold values from 0.15 to 0.45
- buoyancy_freq2: float32 [64], replicated, may hold values from 0.05 to 0.5
Outputs:
- advanced_state: float32 [5, 64, 128, 1024], P(None, None, 'gx', 'gy')
The draws below stay inside these ranges and needn't reach their ends.
Inputs may be any that keep to these rules, and one draw needn't show every extreme that they name: The lengths sum to 1024; block b covers rows block_start[b] to block_start[b] + block_rows[b] - 1 of the strip. Block b lies in slot block_slot[b]; slot q is held by the index q // 2 of gy.
All inputs are finite; a program needn't handle non-finite values.
Results may differ from the reference program's by a relative error of at most 0.00002.
Values sent between devices are 32-bit elements; how exact they have to be, the bound alone decides.
A program may use at most 320 MiB of HBM per device.

```python
import math
import jax
import jax.numpy as jnp
import numpy as np
from jax import lax

FIELDS = 5
LEVELS = 64
SMAX = 16
NSUB = 2
NX = 128
NY = 1024
NBLK = 16
BMAX = 128


def draw_state(key, part):
    rough_key = jax.random.fold_in(jax.random.fold_in(key, 11), 0)
    return jnp.clip(jax.random.normal(rough_key, (FIELDS, LEVELS, NX, NY), jnp.float32), -4.0, 4.0)


def shard_levels(own_key, dims, cuts, smallest, top_value):
    loudness, own = 1.0, jax.random.fold_in(own_key, 6)
    for position, parts in cuts:
        heights = jnp.exp(jax.random.uniform(jax.random.fold_in(own, position), (parts,), jnp.float32, smallest / len(cuts), top_value / len(cuts)))
        loudness = loudness * jnp.repeat(heights, dims[position] // parts).reshape([-1 if axis == position else 1 for axis in range(len(dims))])
    return loudness


def length_profile(number_of, total, most, lean):
    loads = [(1 << 20) // math.isqrt(standing ** lean) + 1 for standing in range(2, number_of + 1)]
    spare, given = total - most - (number_of - 1), [1] * (number_of - 1)
    while spare > 0:
        free = [i for i in range(number_of - 1) if given[i] < most]
        mass, budget = sum([loads[i] for i in free]), spare
        for i in free:
            extra = min(most - given[i], max(1, budget * loads[i] // mass), spare)
            given[i] = given[i] + extra
            spare = spare - extra
    return np.array([most] + given)


def uneven(key, count, total, reach, skew):
    if count == 2:
        one = jax.random.randint(key, (), max(1, total - reach), min(reach, total - 1) + 1)
        return jnp.stack([one, total - one])
    lengths = jnp.asarray(length_profile(count, total, reach, skew), jnp.int32)
    twos = (count - 1) // 2
    giver, sink = lengths[1:1 + 2 * twos:2], lengths[2:2 + 2 * twos:2]
    room = jnp.minimum(giver - 1, reach - sink)
    moved = jax.random.randint(jax.random.fold_in(key, 1), (twos,), 0, 1 << 20) % (room + 1)
    lengths = lengths.at[1:1 + 2 * twos:2].set(giver - moved).at[2:2 + 2 * twos:2].set(sink + moved)
    return lengths[jax.random.permutation(jax.random.fold_in(key, 2), count)]


def gaussian(key, dims, deviation, most, shards=(), held_as=jnp.bfloat16):
    drawn = deviation * jax.random.normal(key, dims, jnp.float32)
    if shards:
        drawn = drawn * shard_levels(key, dims, shards, -0.22, 0.18)
    return jnp.clip(drawn, -most, most).astype(held_as)


def setup_inputs(seed: int = 0) -> dict:
    seeds = jax.random.split(jax.random.key(seed), 8)
    state = draw_state(jax.random.fold_in(seeds[7], 71), 0)
    parent_slots = gaussian(seeds[1], (NBLK, FIELDS, LEVELS, SMAX, BMAX), 1.0, 6.0, ((0, 8),), jnp.float32)
    block_rows = uneven(seeds[2], NBLK, NY, BMAX, 1).astype(jnp.int32)
    block_slot = jax.random.permutation(seeds[3], NBLK).astype(jnp.int32)
    nest_shift = jax.random.randint(seeds[4], (1,), 1, SMAX + 1).astype(jnp.int32)
    sound_speed2 = jnp.clip(jnp.exp(jax.random.uniform(seeds[5], (LEVELS,), jnp.float32, math.log(0.15), math.log(0.45))), 0.15, 0.45)
    buoyancy_freq2 = jnp.clip(jnp.exp(jax.random.uniform(seeds[6], (LEVELS,), jnp.float32, math.log(0.05), math.log(0.5))), 0.05, 0.5)
    return dict(state=state, parent_slots=parent_slots, block_rows=block_rows, block_slot=block_slot, nest_shift=nest_shift, sound_speed2=sound_speed2, buoyancy_freq2=buoyancy_freq2)


def column_update(vert_w, pressure, buoyancy, diverge, sound_speed2, buoyancy_freq2):
    speed_sq = sound_speed2
    press_pred = pressure - speed_sq[:, None, None] * diverge
    buoy_above = jnp.concatenate([buoyancy[1:], jnp.zeros_like(buoyancy[:1])], 0)
    press_above = jnp.concatenate([press_pred[1:], jnp.zeros_like(press_pred[:1])], 0)
    right_side = vert_w + 0.5 * (buoyancy + buoy_above) - (press_above - press_pred)
    speed_above = jnp.concatenate([speed_sq[1:], jnp.zeros_like(speed_sq[:1])], 0)
    diagonal = 1.0 + speed_sq + speed_above
    levels = speed_sq.shape[0]
    ratios = []
    values = []
    divisor = diagonal[0]
    ratios.append(-speed_above[0] / divisor)
    values.append(right_side[0] / divisor)
    for height in range(1, levels):
        divisor = diagonal[height] + speed_sq[height] * ratios[-1]
        ratios.append(-speed_above[height] / divisor)
        values.append((right_side[height] + speed_sq[height] * values[-1]) / divisor)
    solved = [values[-1]]
    for height in range(levels - 2, -1, -1):
        solved.append(values[height] - ratios[height] * solved[-1])
    new_w = jnp.stack(solved[::-1], 0)
    w_below = jnp.concatenate([jnp.zeros_like(new_w[:1]), new_w[:-1]], 0)
    new_p = press_pred - speed_sq[:, None, None] * (new_w - w_below)
    new_b = buoyancy - buoyancy_freq2[:, None, None] * (0.5 * (new_w + w_below))
    return new_w, new_p, new_b


def parent_strip(parent_slots, block_rows, block_slot):
    starts = (jnp.cumsum(block_rows) - block_rows).astype(jnp.int32)
    rows_y = jnp.arange(NY, dtype=jnp.int32)
    owner_block = (jnp.sum((starts[None, :] <= rows_y[:, None]).astype(jnp.int32), axis=1) - 1).astype(jnp.int32)
    offset = (rows_y - starts[owner_block]).astype(jnp.int32)
    slot_y = block_slot[owner_block].astype(jnp.int32)
    picked = parent_slots[slot_y, :, :, :, offset]
    return jnp.moveaxis(picked, 0, 3)


def reference(state, parent_slots, block_rows, block_slot, nest_shift, sound_speed2, buoyancy_freq2):
    edge_strip = parent_strip(parent_slots, block_rows, block_slot)
    extended = jnp.concatenate([state, edge_strip], axis=2)
    shifted = lax.dynamic_slice_in_dim(extended, nest_shift[0].astype(jnp.int32), NX, 2)
    east_u = shifted[0]
    north_v = shifted[1]
    vert_w = shifted[2]
    pressure = shifted[3]
    buoyancy = shifted[4]
    for substep in range(NSUB):
        zeros_x = jnp.zeros_like(pressure[:, :1, :])
        zeros_y = jnp.zeros_like(pressure[:, :, :1])
        pres_east = jnp.concatenate([pressure[:, 1:, :], zeros_x], 1)
        pres_north = jnp.concatenate([pressure[:, :, 1:], zeros_y], 2)
        east_u = east_u - (pres_east - pressure)
        north_v = north_v - (pres_north - pressure)
        west_u = jnp.concatenate([zeros_x, east_u[:, :-1, :]], 1)
        south_v = jnp.concatenate([zeros_y, north_v[:, :, :-1]], 2)
        diverge = (east_u - west_u) + (north_v - south_v)
        vert_w, pressure, buoyancy = column_update(vert_w, pressure, buoyancy, diverge, sound_speed2, buoyancy_freq2)
    return jnp.stack([east_u, north_v, vert_w, pressure, buoyancy], 0)
```

```python
import functools

import jax
import jax.numpy as jnp
from jax import lax
from jax.experimental import pallas as pl
from jax.experimental.pallas import tpu as pltpu
from jax.sharding import PartitionSpec as P

NSUB = 2
MESH = pl.DeviceIdType.MESH


def place_kernel(first_ref, rows_ref, block_ref, slots_ref, out_ref):
    slots, part, strip, lanes = slots_ref.shape
    tiles = out_ref.shape[0]
    lane = lax.broadcasted_iota(jnp.int32, (1, lanes), 1)
    rolled = []
    for slot in range(slots):
        flat = slots_ref[slot].reshape(part * strip, lanes)
        rolled.append(pltpu.roll(flat, lax.rem(first_ref[slot], lanes), 1))
    for tile in range(tiles):
        placed = jnp.zeros((part * strip, lanes), jnp.float32)
        for slot in range(slots):
            offset = lane + (tile * lanes - first_ref[slot])
            inside = (offset >= 0) & (offset < rows_ref[slot])
            placed = jnp.where(inside, rolled[slot], placed)
        out_ref[tile, pl.ds(pl.program_id(0) * part, part)] = placed.reshape(part, strip, lanes)


def place_blocks(slot_rows, firsts, rows, share_index, share, tiles, wanted):
    slots, _, _, lanes = slot_rows.shape
    part = share
    for size in (16, 20, 8, 10, 4, 5, 2, 1):
        if share % size == 0:
            part = size
            break
    steps = share // part
    grid_spec = pltpu.PrefetchScalarGridSpec(
        num_scalar_prefetch=3,
        grid=(steps,),
        in_specs=[
            pl.BlockSpec((slots, part, wanted, lanes), lambda i, f, r, b: (0, b[0] * steps + i, 0, 0))
        ],
        out_specs=pl.BlockSpec(memory_space=pltpu.VMEM),
    )
    return pl.pallas_call(
        place_kernel,
        grid_spec=grid_spec,
        out_shape=jax.ShapeDtypeStruct((tiles, share, wanted, lanes), jnp.float32),
        compiler_params=pltpu.CompilerParams(vmem_limit_bytes=16 * 1024 * 1024),
        name="place_blocks",
    )(firsts, rows, share_index, slot_rows)


def scatter_kernel(ny, placed_ref, out_ref, up, down, up_send, up_recv, down_send, down_recv):
    gx = lax.axis_index("gx")
    gy = lax.axis_index("gy")
    has_south, has_north = gy > 0, gy < ny - 1
    south, north = (gx, gy - 1), (gx, gy + 1)

    barrier = pltpu.get_barrier_semaphore()
    for exists, peer in ((has_south, south), (has_north, north)):
        @pl.when(exists)
        def _(peer=peer):
            pl.semaphore_signal(barrier, inc=1, device_id=peer, device_id_type=MESH)
    pl.semaphore_wait(barrier, has_south.astype(jnp.int32) + has_north.astype(jnp.int32))

    def hop(source, target, sends, receives, tile, peer):
        return pltpu.make_async_remote_copy(
            src_ref=source.at[tile],
            dst_ref=target.at[tile],
            send_sem=sends.at[tile],
            recv_sem=receives.at[tile],
            device_id=peer,
            device_id_type=MESH,
        )

    lines = (
        (up, up_send, up_recv, north, has_south, has_north),
        (down, down_send, down_recv, south, has_north, has_south),
    )

    def tile_at(line, step):
        return ny - 1 - (step - gy) if line == 0 else step - (ny - 1 - gy)

    for step in range(ny - 1):
        for line, (held, sends, receives, peer, has_before, has_after) in enumerate(lines):
            tile = tile_at(line, step)
            active = has_after & ((step >= gy) if line == 0 else (step >= ny - 1 - gy))

            @pl.when(active & has_before)
            def _(held=held, sends=sends, receives=receives, peer=peer, tile=tile):
                copy = hop(held, held, sends, receives, tile, peer)
                copy.wait_recv()
                held[tile] = held[tile] + placed_ref[tile]
                copy.start()

            @pl.when(active & jnp.logical_not(has_before))
            def _(held=held, sends=sends, receives=receives, peer=peer, tile=tile):
                hop(placed_ref, held, sends, receives, tile, peer).start()

    out_ref[...] = placed_ref[gy]
    for held, sends, receives, peer, has_before, _ in lines:
        @pl.when(has_before)
        def _(held=held, sends=sends, receives=receives, peer=peer):
            hop(held, held, sends, receives, gy, peer).wait_recv()
            out_ref[...] = out_ref[...] + held[gy]

    for step in range(ny - 1):
        for line, (held, sends, receives, peer, has_before, has_after) in enumerate(lines):
            tile = tile_at(line, step)
            active = has_after & ((step >= gy) if line == 0 else (step >= ny - 1 - gy))

            @pl.when(active)
            def _(held=held, sends=sends, receives=receives, peer=peer, tile=tile):
                hop(held, held, sends, receives, tile, peer).wait_send()


def scatter(placed, kernel_id):
    ny = placed.shape[0]
    size = placed.size * 4
    vmem = pl.BlockSpec(memory_space=pltpu.VMEM)
    return pl.pallas_call(
        functools.partial(scatter_kernel, ny),
        out_shape=jax.ShapeDtypeStruct(placed.shape[1:], jnp.float32),
        in_specs=[vmem],
        out_specs=vmem,
        scratch_shapes=[
            pltpu.VMEM(placed.shape, jnp.float32),
            pltpu.VMEM(placed.shape, jnp.float32),
            pltpu.SemaphoreType.DMA((ny,)),
            pltpu.SemaphoreType.DMA((ny,)),
            pltpu.SemaphoreType.DMA((ny,)),
            pltpu.SemaphoreType.DMA((ny,)),
        ],
        compiler_params=pltpu.CompilerParams(
            collective_id=kernel_id, has_side_effects=True, vmem_limit_bytes=40 * 1024 * 1024
        ),
        cost_estimate=pl.CostEstimate(flops=0, bytes_accessed=40 * size, transcendentals=0),
        name="scatter_line",
    )(placed)


def advance_kernel(
    nx, ny, levels, shift_ref, speed_ref, freq_ref, state_ref, beyond_ref, piece_ref, out_ref,
    ext, inv, ratio, send_x, recv_x, send_y, recv_y,
    local_sem, piece_send, piece_recv, halo_send, halo_recv,
):
    gx = lax.axis_index("gx")
    gy = lax.axis_index("gy")
    cols, lanes = out_ref.shape[1], out_ref.shape[2]
    strip = ext.shape[1] - cols
    share = piece_ref.shape[0]
    has_west, has_east = gx > 0, gx < nx - 1
    has_south, has_north = gy > 0, gy < ny - 1
    at_edge = gx == nx - 1
    peers = (
        (has_west, (gx - 1, gy)),
        (has_east, (gx + 1, gy)),
        (has_south, (gx, gy - 1)),
        (has_north, (gx, gy + 1)),
    )

    own_copy = pltpu.make_async_copy(state_ref, ext.at[:, pl.ds(0, cols), :], local_sem.at[0])
    own_copy.start()
    beyond_copy = pltpu.make_async_copy(beyond_ref, ext.at[:, pl.ds(cols, strip), :], local_sem.at[1])

    @pl.when(jnp.logical_not(at_edge))
    def _():
        beyond_copy.start()

    barrier = pltpu.get_barrier_semaphore()
    for exists, peer in peers:
        @pl.when(exists)
        def _(peer=peer):
            pl.semaphore_signal(barrier, inc=1, device_id=peer, device_id_type=MESH)

    @pl.when(jnp.logical_not(at_edge))
    def _():
        pl.semaphore_signal(barrier, inc=1, device_id=(nx - 1, gy), device_id_type=MESH)

    @pl.when(at_edge)
    def _():
        for other in range(nx - 1):
            pl.semaphore_signal(barrier, inc=1, device_id=(other, gy), device_id_type=MESH)

    greeted = sum(exists.astype(jnp.int32) for exists, _ in peers)
    pl.semaphore_wait(barrier, greeted + jnp.where(at_edge, nx - 1, 1))

    def piece_copy(source):
        return pltpu.make_async_remote_copy(
            src_ref=piece_ref,
            dst_ref=ext.at[pl.ds(source * share, share), pl.ds(cols, strip), :],
            send_sem=piece_send,
            recv_sem=piece_recv.at[source],
            device_id=(nx - 1, gy),
            device_id_type=MESH,
        )

    own_piece = pltpu.make_async_copy(
        piece_ref, ext.at[pl.ds((nx - 1) * share, share), pl.ds(cols, strip), :], local_sem.at[1]
    )
    for source in range(nx - 1):
        @pl.when(gx == source)
        def _(source=source):
            piece_copy(source).start()

    @pl.when(at_edge)
    def _():
        own_piece.start()

    def coefficients(k, before):
        speed = speed_ref[k]
        above = speed_ref[k + 1]
        inverse = 1.0 / ((1.0 + speed + above) + speed * before)
        inv[k] = inverse
        now = -above * inverse
        ratio[k] = now
        return now

    lax.fori_loop(0, levels, coefficients, jnp.zeros((8, lanes), jnp.float32))

    own_copy.wait()

    @pl.when(jnp.logical_not(at_edge))
    def _():
        beyond_copy.wait()

    @pl.when(at_edge)
    def _():
        own_piece.wait()
        for source in range(nx - 1):
            piece_copy(source).wait_recv()

    shift = shift_ref[0]
    row = lax.broadcasted_iota(jnp.int32, (cols, lanes), 0)
    lane = lax.broadcasted_iota(jnp.int32, (cols, lanes), 1)
    west_on = has_west.astype(jnp.float32)
    east_on = has_east.astype(jnp.float32)
    south_on = has_south.astype(jnp.float32)
    north_on = has_north.astype(jnp.float32)
    wide = (cols, lanes)

    def collect(sub, k, u, v, p, packs):
        low, high = packs
        send_x[sub, 0, pl.ds(k, 1), :] = p[0:1, :]
        send_x[sub, 1, pl.ds(k, 1), :] = u[cols - 1:cols, :] + p[cols - 1:cols, :]
        sums = v + p
        low = jnp.where(lane == k, jnp.broadcast_to(p[:, 0:1], wide), low)
        high = jnp.where(lane == k, jnp.broadcast_to(sums[:, lanes - 1:lanes], wide), high)
        return low, high

    def halo_copies(sub):
        def one(source, target, index, peer):
            return pltpu.make_async_remote_copy(
                src_ref=source.at[sub, index % 2],
                dst_ref=target.at[sub, index % 2],
                send_sem=halo_send.at[sub, index],
                recv_sem=halo_recv.at[sub, index],
                device_id=peer,
                device_id_type=MESH,
            )
        return (
            (has_west, has_east, one(send_x, recv_x, 0, (gx - 1, gy))),
            (has_east, has_west, one(send_x, recv_x, 1, (gx + 1, gy))),
            (has_south, has_north, one(send_y, recv_y, 2, (gx, gy - 1))),
            (has_north, has_south, one(send_y, recv_y, 3, (gx, gy + 1))),
        )

    def exchange(sub, packs):
        send_y[sub, 0] = packs[0]
        send_y[sub, 1] = packs[1]
        for sends, _, copy in halo_copies(sub):
            pl.when(sends)(copy.start)
        for sends, receives, copy in halo_copies(sub):
            pl.when(sends)(copy.wait_send)
            pl.when(receives)(copy.wait_recv)

    no_packs = (jnp.zeros(wide, jnp.float32), jnp.zeros(wide, jnp.float32))

    def assemble(k, packs):
        fields = []
        for field in range(5):
            value = ext[field * levels + k, pl.ds(shift, cols), :]
            out_ref[field * levels + k] = value
            fields.append(value)
        return collect(0, k, fields[0], fields[1], fields[3], packs)

    packs = lax.fori_loop(0, levels, assemble, no_packs, unroll=2)
    U, V, W, PR, G = (field * levels for field in range(5))

    def mul(scale, value):
        return (scale[None] * value.reshape(cols // 8, 8, lanes)).reshape(cols, lanes)

    for sub in range(NSUB):
        exchange(sub, packs)
        clear_x = jnp.zeros((levels, lanes), jnp.float32)
        for exists, index in ((has_east, 0), (has_west, 1)):
            @pl.when(jnp.logical_not(exists))
            def _(index=index):
                recv_x[sub, index] = clear_x
        for exists, index in ((has_north, 0), (has_south, 1)):
            @pl.when(jnp.logical_not(exists))
            def _(index=index):
                recv_y[sub, index] = jnp.zeros(wide, jnp.float32)
        north0 = pltpu.roll(recv_y[sub, 0], lanes - 1, 1)
        south0 = recv_y[sub, 1]

        def predict(k, north, south):
            u, v, p = out_ref[U + k], out_ref[V + k], out_ref[PR + k]
            p_east = jnp.where(row == cols - 1, recv_x[sub, 0, pl.ds(k, 1), :], pltpu.roll(p, cols - 1, 0))
            p_north = jnp.where(lane == lanes - 1, north, pltpu.roll(p, lanes - 1, 1))
            west_edge = (recv_x[sub, 1, pl.ds(k, 1), :] - p[0:1, :]) * west_on
            south_edge = (south - p) * south_on
            u = u - (p_east - p)
            v = v - (p_north - p)
            u_west = jnp.where(row == 0, west_edge, pltpu.roll(u, 1, 0))
            v_south = jnp.where(lane == 0, south_edge, pltpu.roll(v, 1, 1))
            out_ref[U + k] = u
            out_ref[V + k] = v
            star = p - speed_ref[k] * ((u - u_west) + (v - v_south))
            out_ref[PR + k] = star
            return star, pltpu.roll(north, lanes - 1, 1), pltpu.roll(south, lanes - 1, 1)

        def eliminate(k, star, star_above, g, g_above, value):
            right = out_ref[W + k] + 0.5 * (g + g_above) - (star_above - star)
            value = mul(inv[k], right + speed_ref[k] * value)
            out_ref[W + k] = value
            return value

        star, north, south = predict(0, north0, south0)

        def forward(k, carry):
            star, g, value, north, south = carry
            star_above, north, south = predict(k, north, south)
            g_above = out_ref[G + k]
            value = eliminate(k - 1, star, star_above, g, g_above, value)
            return star_above, g_above, value, north, south

        zero = jnp.zeros(wide, jnp.float32)
        carry = lax.fori_loop(1, levels, forward, (star, out_ref[G], zero, north, south), unroll=3)
        star, g, value = carry[:3]
        w_top = eliminate(levels - 1, star, zero, g, zero, value)

        def finish(k, w, w_below, packs):
            p = out_ref[PR + k] - speed_ref[k] * (w - w_below)
            out_ref[PR + k] = p
            out_ref[G + k] = out_ref[G + k] - freq_ref[k] * (0.5 * (w + w_below))
            if sub < NSUB - 1:
                packs = collect(sub + 1, k, out_ref[U + k], out_ref[V + k], p, packs)
            return packs

        def backward(step, carry):
            w, packs = carry
            k = levels - 2 - step
            w_below = out_ref[W + k] - mul(ratio[k], w)
            out_ref[W + k] = w_below
            return w_below, finish(k + 1, w, w_below, packs)

        w, packs = lax.fori_loop(0, levels - 1, backward, (w_top, no_packs), unroll=3)
        packs = finish(0, w, zero, packs)

    for source in range(nx - 1):
        @pl.when(gx == source)
        def _(source=source):
            piece_copy(source).wait_send()


def advance(state, beyond, piece, nest_shift, sound_speed2, buoyancy_freq2, levels, kernel_id):
    nx, ny = lax.axis_size("gx"), lax.axis_size("gy")
    rows, cols, lanes = state.shape
    strip = beyond.shape[1]
    speed = jnp.concatenate([sound_speed2, jnp.zeros((1,), jnp.float32)])
    smem = pl.BlockSpec(memory_space=pltpu.SMEM)
    hbm = pl.BlockSpec(memory_space=pl.ANY)
    return pl.pallas_call(
        functools.partial(advance_kernel, nx, ny, levels),
        out_shape=jax.ShapeDtypeStruct(state.shape, jnp.float32),
        in_specs=[smem, smem, smem, hbm, hbm, hbm],
        out_specs=pl.BlockSpec(memory_space=pltpu.VMEM),
        scratch_shapes=[
            pltpu.VMEM((rows, cols + strip, lanes), jnp.float32),
            pltpu.VMEM((levels, 8, lanes), jnp.float32),
            pltpu.VMEM((levels, 8, lanes), jnp.float32),
            pltpu.VMEM((NSUB, 2, levels, lanes), jnp.float32),
            pltpu.VMEM((NSUB, 2, levels, lanes), jnp.float32),
            pltpu.VMEM((NSUB, 2, cols, lanes), jnp.float32),
            pltpu.VMEM((NSUB, 2, cols, lanes), jnp.float32),
            pltpu.SemaphoreType.DMA((2,)),
            pltpu.SemaphoreType.DMA,
            pltpu.SemaphoreType.DMA((nx,)),
            pltpu.SemaphoreType.DMA((NSUB, 4)),
            pltpu.SemaphoreType.DMA((NSUB, 4)),
        ],
        compiler_params=pltpu.CompilerParams(
            collective_id=kernel_id, has_side_effects=True, vmem_limit_bytes=40 * 1024 * 1024
        ),
        name="advance",
    )(nest_shift, speed, buoyancy_freq2, state, beyond, piece)


def program(wanted, kernel_id, state, parent_slots, block_rows, block_slot, nest_shift, sound_speed2, buoyancy_freq2):
    fields, levels, cols_x, cols_y = state.shape
    slots, _, _, strip, most = parent_slots.shape
    nx, ny = lax.axis_size("gx"), lax.axis_size("gy")
    flat = state.reshape(fields * levels, cols_x, cols_y)
    route = [(i, i - 1) for i in range(1, nx)]
    beyond = lax.ppermute(flat[:, :wanted, :], "gx", route)

    total = block_slot.shape[0]
    ordinal = jnp.arange(total, dtype=jnp.int32)
    mine = lax.axis_index("gy") * slots + jnp.arange(slots, dtype=jnp.int32)
    is_mine = block_slot[None, :] == mine[:, None]
    before = ordinal[None, :] < ordinal[:, None]
    starts = jnp.sum(jnp.where(before, block_rows[None, :], 0), axis=1)
    firsts = jnp.sum(jnp.where(is_mine, starts[None, :], 0), axis=1)
    rows = jnp.sum(jnp.where(is_mine, block_rows[None, :], 0), axis=1)
    share = fields * levels // nx
    share_index = lax.axis_index("gx").astype(jnp.int32).reshape(1)
    placed = place_blocks(
        parent_slots.reshape(slots, fields * levels, strip, most), firsts, rows, share_index, share, ny, wanted
    )
    piece = scatter(placed, kernel_id + 2)
    out = advance(flat, beyond, piece, nest_shift, sound_speed2, buoyancy_freq2, levels, kernel_id)
    return out.reshape(state.shape)


def shards(*args):
    strip, shift = args[1].shape[3], args[4]
    half = strip // 2
    if half % 8:
        return program(strip, 0, *args)
    return lax.cond(
        shift[0] <= half, functools.partial(program, half, 0), functools.partial(program, strip, 1), *args
    )


def solution(mesh):
    placed = (P(None, None, "gx", "gy"), P("gy", None, None, None, None), P(), P(), P(), P(), P())
    return jax.shard_map(
        shards, mesh=mesh, in_specs=placed, out_specs=P(None, None, "gx", "gy"), check_vma=False
    )
```

```python
import functools

import jax
import jax.numpy as jnp
from jax import lax
from jax.experimental import pallas as pl
from jax.experimental.pallas import tpu as pltpu
from jax.sharding import PartitionSpec as P

NSUB = 2
MESH = pl.DeviceIdType.MESH


def place_kernel(first_ref, rows_ref, block_ref, slots_ref, out_ref):
    slots, part, strip, lanes = slots_ref.shape
    tiles = out_ref.shape[0]
    lane = lax.broadcasted_iota(jnp.int32, (1, lanes), 1)
    rolled = []
    for slot in range(slots):
        flat = slots_ref[slot].reshape(part * strip, lanes)
        rolled.append(pltpu.roll(flat, lax.rem(first_ref[slot], lanes), 1))
    for tile in range(tiles):
        placed = jnp.zeros((part * strip, lanes), jnp.float32)
        for slot in range(slots):
            offset = lane + (tile * lanes - first_ref[slot])
            inside = (offset >= 0) & (offset < rows_ref[slot])
            placed = jnp.where(inside, rolled[slot], placed)
        out_ref[tile, pl.ds(pl.program_id(0) * part, part)] = placed.reshape(part, strip, lanes)


def place_blocks(slot_rows, firsts, rows, share_index, share, tiles, wanted):
    slots, _, _, lanes = slot_rows.shape
    part = share
    for size in (16, 20, 8, 10, 4, 5, 2, 1):
        if share % size == 0:
            part = size
            break
    steps = share // part
    grid_spec = pltpu.PrefetchScalarGridSpec(
        num_scalar_prefetch=3,
        grid=(steps,),
        in_specs=[
            pl.BlockSpec((slots, part, wanted, lanes), lambda i, f, r, b: (0, b[0] * steps + i, 0, 0))
        ],
        out_specs=pl.BlockSpec(memory_space=pltpu.VMEM),
    )
    return pl.pallas_call(
        place_kernel,
        grid_spec=grid_spec,
        out_shape=jax.ShapeDtypeStruct((tiles, share, wanted, lanes), jnp.float32),
        compiler_params=pltpu.CompilerParams(vmem_limit_bytes=16 * 1024 * 1024),
        name="place_blocks",
    )(firsts, rows, share_index, slot_rows)


def scatter_kernel(ny, placed_ref, out_ref, up, down, up_send, up_recv, down_send, down_recv):
    gx = lax.axis_index("gx")
    gy = lax.axis_index("gy")
    has_south, has_north = gy > 0, gy < ny - 1
    south, north = (gx, gy - 1), (gx, gy + 1)

    barrier = pltpu.get_barrier_semaphore()
    for exists, peer in ((has_south, south), (has_north, north)):
        @pl.when(exists)
        def _(peer=peer):
            pl.semaphore_signal(barrier, inc=1, device_id=peer, device_id_type=MESH)
    pl.semaphore_wait(barrier, has_south.astype(jnp.int32) + has_north.astype(jnp.int32))

    def hop(source, target, sends, receives, tile, peer):
        return pltpu.make_async_remote_copy(
            src_ref=source.at[tile],
            dst_ref=target.at[tile],
            send_sem=sends.at[tile],
            recv_sem=receives.at[tile],
            device_id=peer,
            device_id_type=MESH,
        )

    lines = (
        (up, up_send, up_recv, north, has_south, has_north),
        (down, down_send, down_recv, south, has_north, has_south),
    )

    def tile_at(line, step):
        return ny - 1 - (step - gy) if line == 0 else step - (ny - 1 - gy)

    for step in range(ny - 1):
        for line, (held, sends, receives, peer, has_before, has_after) in enumerate(lines):
            tile = tile_at(line, step)
            active = has_after & ((step >= gy) if line == 0 else (step >= ny - 1 - gy))

            @pl.when(active & has_before)
            def _(held=held, sends=sends, receives=receives, peer=peer, tile=tile):
                copy = hop(held, held, sends, receives, tile, peer)
                copy.wait_recv()
                held[tile] = held[tile] + placed_ref[tile]
                copy.start()

            @pl.when(active & jnp.logical_not(has_before))
            def _(held=held, sends=sends, receives=receives, peer=peer, tile=tile):
                hop(placed_ref, held, sends, receives, tile, peer).start()

    out_ref[...] = placed_ref[gy]
    for held, sends, receives, peer, has_before, _ in lines:
        @pl.when(has_before)
        def _(held=held, sends=sends, receives=receives, peer=peer):
            hop(held, held, sends, receives, gy, peer).wait_recv()
            out_ref[...] = out_ref[...] + held[gy]

    for step in range(ny - 1):
        for line, (held, sends, receives, peer, has_before, has_after) in enumerate(lines):
            tile = tile_at(line, step)
            active = has_after & ((step >= gy) if line == 0 else (step >= ny - 1 - gy))

            @pl.when(active)
            def _(held=held, sends=sends, receives=receives, peer=peer, tile=tile):
                hop(held, held, sends, receives, tile, peer).wait_send()


def scatter(placed, kernel_id):
    ny = placed.shape[0]
    size = placed.size * 4
    vmem = pl.BlockSpec(memory_space=pltpu.VMEM)
    return pl.pallas_call(
        functools.partial(scatter_kernel, ny),
        out_shape=jax.ShapeDtypeStruct(placed.shape[1:], jnp.float32),
        in_specs=[vmem],
        out_specs=vmem,
        scratch_shapes=[
            pltpu.VMEM(placed.shape, jnp.float32),
            pltpu.VMEM(placed.shape, jnp.float32),
            pltpu.SemaphoreType.DMA((ny,)),
            pltpu.SemaphoreType.DMA((ny,)),
            pltpu.SemaphoreType.DMA((ny,)),
            pltpu.SemaphoreType.DMA((ny,)),
        ],
        compiler_params=pltpu.CompilerParams(
            collective_id=kernel_id, has_side_effects=True, vmem_limit_bytes=40 * 1024 * 1024
        ),
        cost_estimate=pl.CostEstimate(flops=0, bytes_accessed=40 * size, transcendentals=0),
        name="scatter_line",
    )(placed)


def advance_kernel(
    nx, ny, levels, shift_ref, speed_ref, freq_ref, state_ref, beyond_ref, piece_ref, out_ref,
    ext, inv, ratio, send_x, recv_x, send_y, recv_y,
    local_sem, piece_send, piece_recv, halo_send, halo_recv,
):
    gx = lax.axis_index("gx")
    gy = lax.axis_index("gy")
    cols, lanes = out_ref.shape[1], out_ref.shape[2]
    strip = ext.shape[1] - cols
    share = piece_ref.shape[0]
    has_west, has_east = gx > 0, gx < nx - 1
    has_south, has_north = gy > 0, gy < ny - 1
    at_edge = gx == nx - 1
    peers = (
        (has_west, (gx - 1, gy)),
        (has_east, (gx + 1, gy)),
        (has_south, (gx, gy - 1)),
        (has_north, (gx, gy + 1)),
    )

    own_copy = pltpu.make_async_copy(state_ref, ext.at[:, pl.ds(0, cols), :], local_sem.at[0])
    own_copy.start()
    beyond_copy = pltpu.make_async_copy(beyond_ref, ext.at[:, pl.ds(cols, strip), :], local_sem.at[1])

    @pl.when(jnp.logical_not(at_edge))
    def _():
        beyond_copy.start()

    barrier = pltpu.get_barrier_semaphore()
    for exists, peer in peers:
        @pl.when(exists)
        def _(peer=peer):
            pl.semaphore_signal(barrier, inc=1, device_id=peer, device_id_type=MESH)

    @pl.when(jnp.logical_not(at_edge))
    def _():
        pl.semaphore_signal(barrier, inc=1, device_id=(nx - 1, gy), device_id_type=MESH)

    @pl.when(at_edge)
    def _():
        for other in range(nx - 1):
            pl.semaphore_signal(barrier, inc=1, device_id=(other, gy), device_id_type=MESH)

    greeted = sum(exists.astype(jnp.int32) for exists, _ in peers)
    pl.semaphore_wait(barrier, greeted + jnp.where(at_edge, nx - 1, 1))

    def piece_copy(source):
        return pltpu.make_async_remote_copy(
            src_ref=piece_ref,
            dst_ref=ext.at[pl.ds(source * share, share), pl.ds(cols, strip), :],
            send_sem=piece_send,
            recv_sem=piece_recv.at[source],
            device_id=(nx - 1, gy),
            device_id_type=MESH,
        )

    own_piece = pltpu.make_async_copy(
        piece_ref, ext.at[pl.ds((nx - 1) * share, share), pl.ds(cols, strip), :], local_sem.at[1]
    )
    for source in range(nx - 1):
        @pl.when(gx == source)
        def _(source=source):
            piece_copy(source).start()

    @pl.when(at_edge)
    def _():
        own_piece.start()

    def coefficients(k, before):
        speed = speed_ref[k]
        above = speed_ref[k + 1]
        inverse = 1.0 / ((1.0 + speed + above) + speed * before)
        inv[k] = inverse
        now = -above * inverse
        ratio[k] = now
        return now

    lax.fori_loop(0, levels, coefficients, jnp.zeros((8, lanes), jnp.float32))

    own_copy.wait()

    @pl.when(jnp.logical_not(at_edge))
    def _():
        beyond_copy.wait()

    @pl.when(at_edge)
    def _():
        own_piece.wait()
        for source in range(nx - 1):
            piece_copy(source).wait_recv()

    shift = shift_ref[0]
    row = lax.broadcasted_iota(jnp.int32, (cols, lanes), 0)
    lane = lax.broadcasted_iota(jnp.int32, (cols, lanes), 1)
    west_on = has_west.astype(jnp.float32)
    east_on = has_east.astype(jnp.float32)
    south_on = has_south.astype(jnp.float32)
    north_on = has_north.astype(jnp.float32)
    wide = (cols, lanes)

    def collect(sub, k, u, v, p, packs):
        low, high = packs
        send_x[sub, 0, pl.ds(k, 1), :] = p[0:1, :]
        send_x[sub, 1, pl.ds(k, 1), :] = u[cols - 1:cols, :] + p[cols - 1:cols, :]
        sums = v + p
        low = jnp.where(lane == k, jnp.broadcast_to(p[:, 0:1], wide), low)
        high = jnp.where(lane == k, jnp.broadcast_to(sums[:, lanes - 1:lanes], wide), high)
        return low, high

    def halo_copies(sub):
        def one(source, target, index, peer):
            return pltpu.make_async_remote_copy(
                src_ref=source.at[sub, index % 2],
                dst_ref=target.at[sub, index % 2],
                send_sem=halo_send.at[sub, index],
                recv_sem=halo_recv.at[sub, index],
                device_id=peer,
                device_id_type=MESH,
            )
        return (
            (has_west, has_east, one(send_x, recv_x, 0, (gx - 1, gy))),
            (has_east, has_west, one(send_x, recv_x, 1, (gx + 1, gy))),
            (has_south, has_north, one(send_y, recv_y, 2, (gx, gy - 1))),
            (has_north, has_south, one(send_y, recv_y, 3, (gx, gy + 1))),
        )

    def exchange(sub, packs):
        send_y[sub, 0] = packs[0]
        send_y[sub, 1] = packs[1]
        for sends, _, copy in halo_copies(sub):
            pl.when(sends)(copy.start)
        for sends, receives, copy in halo_copies(sub):
            pl.when(sends)(copy.wait_send)
            pl.when(receives)(copy.wait_recv)

    no_packs = (jnp.zeros(wide, jnp.float32), jnp.zeros(wide, jnp.float32))

    def assemble(k, packs):
        fields = []
        for field in range(5):
            value = ext[field * levels + k, pl.ds(shift, cols), :]
            out_ref[field * levels + k] = value
            fields.append(value)
        return collect(0, k, fields[0], fields[1], fields[3], packs)

    packs = lax.fori_loop(0, levels, assemble, no_packs, unroll=4)
    U, V, W, PR, G = (field * levels for field in range(5))

    def mul(scale, value):
        return (scale[None] * value.reshape(cols // 8, 8, lanes)).reshape(cols, lanes)

    for sub in range(NSUB):
        exchange(sub, packs)
        clear_x = jnp.zeros((levels, lanes), jnp.float32)
        for exists, index in ((has_east, 0), (has_west, 1)):
            @pl.when(jnp.logical_not(exists))
            def _(index=index):
                recv_x[sub, index] = clear_x
        for exists, index in ((has_north, 0), (has_south, 1)):
            @pl.when(jnp.logical_not(exists))
            def _(index=index):
                recv_y[sub, index] = jnp.zeros(wide, jnp.float32)
        north0 = pltpu.roll(recv_y[sub, 0], lanes - 1, 1)
        south0 = recv_y[sub, 1]

        def predict(k, north, south):
            u, v, p = out_ref[U + k], out_ref[V + k], out_ref[PR + k]
            p_east = jnp.where(row == cols - 1, recv_x[sub, 0, pl.ds(k, 1), :], pltpu.roll(p, cols - 1, 0))
            p_north = jnp.where(lane == lanes - 1, north, pltpu.roll(p, lanes - 1, 1))
            west_edge = (recv_x[sub, 1, pl.ds(k, 1), :] - p[0:1, :]) * west_on
            south_edge = (south - p) * south_on
            u = u - (p_east - p)
            v = v - (p_north - p)
            u_west = jnp.where(row == 0, west_edge, pltpu.roll(u, 1, 0))
            v_south = jnp.where(lane == 0, south_edge, pltpu.roll(v, 1, 1))
            out_ref[U + k] = u
            out_ref[V + k] = v
            star = p - speed_ref[k] * ((u - u_west) + (v - v_south))
            out_ref[PR + k] = star
            return star, pltpu.roll(north, lanes - 1, 1), pltpu.roll(south, lanes - 1, 1)

        def eliminate(k, star, star_above, g, g_above, value):
            right = out_ref[W + k] + 0.5 * (g + g_above) - (star_above - star)
            value = mul(inv[k], right + speed_ref[k] * value)
            out_ref[W + k] = value
            return value

        star, north, south = predict(0, north0, south0)

        def forward(k, carry):
            star, g, value, north, south = carry
            star_above, north, south = predict(k, north, south)
            g_above = out_ref[G + k]
            value = eliminate(k - 1, star, star_above, g, g_above, value)
            return star_above, g_above, value, north, south

        zero = jnp.zeros(wide, jnp.float32)
        carry = lax.fori_loop(1, levels, forward, (star, out_ref[G], zero, north, south), unroll=7)
        star, g, value = carry[:3]
        w_top = eliminate(levels - 1, star, zero, g, zero, value)

        def finish(k, w, w_below, packs):
            p = out_ref[PR + k] - speed_ref[k] * (w - w_below)
            out_ref[PR + k] = p
            out_ref[G + k] = out_ref[G + k] - freq_ref[k] * (0.5 * (w + w_below))
            if sub < NSUB - 1:
                packs = collect(sub + 1, k, out_ref[U + k], out_ref[V + k], p, packs)
            return packs

        def backward(step, carry):
            w, packs = carry
            k = levels - 2 - step
            w_below = out_ref[W + k] - mul(ratio[k], w)
            out_ref[W + k] = w_below
            return w_below, finish(k + 1, w, w_below, packs)

        w, packs = lax.fori_loop(0, levels - 1, backward, (w_top, no_packs), unroll=7)
        packs = finish(0, w, zero, packs)

    for source in range(nx - 1):
        @pl.when(gx == source)
        def _(source=source):
            piece_copy(source).wait_send()


def advance(state, beyond, piece, nest_shift, sound_speed2, buoyancy_freq2, levels, kernel_id):
    nx, ny = lax.axis_size("gx"), lax.axis_size("gy")
    rows, cols, lanes = state.shape
    strip = beyond.shape[1]
    speed = jnp.concatenate([sound_speed2, jnp.zeros((1,), jnp.float32)])
    smem = pl.BlockSpec(memory_space=pltpu.SMEM)
    hbm = pl.BlockSpec(memory_space=pl.ANY)
    return pl.pallas_call(
        functools.partial(advance_kernel, nx, ny, levels),
        out_shape=jax.ShapeDtypeStruct(state.shape, jnp.float32),
        in_specs=[smem, smem, smem, hbm, hbm, hbm],
        out_specs=pl.BlockSpec(memory_space=pltpu.VMEM),
        scratch_shapes=[
            pltpu.VMEM((rows, cols + strip, lanes), jnp.float32),
            pltpu.VMEM((levels, 8, lanes), jnp.float32),
            pltpu.VMEM((levels, 8, lanes), jnp.float32),
            pltpu.VMEM((NSUB, 2, levels, lanes), jnp.float32),
            pltpu.VMEM((NSUB, 2, levels, lanes), jnp.float32),
            pltpu.VMEM((NSUB, 2, cols, lanes), jnp.float32),
            pltpu.VMEM((NSUB, 2, cols, lanes), jnp.float32),
            pltpu.SemaphoreType.DMA((2,)),
            pltpu.SemaphoreType.DMA,
            pltpu.SemaphoreType.DMA((nx,)),
            pltpu.SemaphoreType.DMA((NSUB, 4)),
            pltpu.SemaphoreType.DMA((NSUB, 4)),
        ],
        compiler_params=pltpu.CompilerParams(
            collective_id=kernel_id, has_side_effects=True, vmem_limit_bytes=40 * 1024 * 1024
        ),
        name="advance",
    )(nest_shift, speed, buoyancy_freq2, state, beyond, piece)


def program(wanted, kernel_id, state, parent_slots, block_rows, block_slot, nest_shift, sound_speed2, buoyancy_freq2):
    fields, levels, cols_x, cols_y = state.shape
    slots, _, _, strip, most = parent_slots.shape
    nx, ny = lax.axis_size("gx"), lax.axis_size("gy")
    flat = state.reshape(fields * levels, cols_x, cols_y)
    route = [(i, i - 1) for i in range(1, nx)]
    beyond = lax.ppermute(flat[:, :wanted, :], "gx", route)

    total = block_slot.shape[0]
    ordinal = jnp.arange(total, dtype=jnp.int32)
    mine = lax.axis_index("gy") * slots + jnp.arange(slots, dtype=jnp.int32)
    is_mine = block_slot[None, :] == mine[:, None]
    before = ordinal[None, :] < ordinal[:, None]
    starts = jnp.sum(jnp.where(before, block_rows[None, :], 0), axis=1)
    firsts = jnp.sum(jnp.where(is_mine, starts[None, :], 0), axis=1)
    rows = jnp.sum(jnp.where(is_mine, block_rows[None, :], 0), axis=1)
    share = fields * levels // nx
    share_index = lax.axis_index("gx").astype(jnp.int32).reshape(1)
    placed = place_blocks(
        parent_slots.reshape(slots, fields * levels, strip, most), firsts, rows, share_index, share, ny, wanted
    )
    piece = scatter(placed, kernel_id + 2)
    out = advance(flat, beyond, piece, nest_shift, sound_speed2, buoyancy_freq2, levels, kernel_id)
    return out.reshape(state.shape)


def shards(*args):
    strip, shift = args[1].shape[3], args[4]
    half = strip // 2
    if half % 8:
        return program(strip, 0, *args)
    return lax.cond(
        shift[0] <= half, functools.partial(program, half, 0), functools.partial(program, strip, 1), *args
    )


def solution(mesh):
    placed = (P(None, None, "gx", "gy"), P("gy", None, None, None, None), P(), P(), P(), P(), P())
    return jax.shard_map(
        shards, mesh=mesh, in_specs=placed, out_specs=P(None, None, "gx", "gy"), check_vma=False
    )
```
